32 devices in a mesh: group: 2 (over x), row: 16 (over z, y, core).
Axes of the slice: x: 2, y: 2, z: 4, core: 2. Of those that a mesh axis runs over, the one named last changes fastest.
Arguments:
- alignment: bfloat16 [256, 128, 256], P(('group', 'row')), parts along dimension 0, may hold values from -6 to 6
- pair_rep: bfloat16 [256, 128, 128], P(('group', 'row')), parts along dimension 0, may hold values from -6 to 6
- alignment_norm_gain: float32 [256], replicated, may hold values from 0.5 to 1.5
- alignment_norm_offset: float32 [256], replicated, may hold values from -3 to 3
- left_projection_weight: bfloat16 [256, 32], replicated, may hold values from -0.375 to 0.375
- right_projection_weight: bfloat16 [256, 32], replicated, may hold values from -0.375 to 0.375
- outer_weight: bfloat16 [1024, 128], replicated, may hold values from -0.75 to 0.75
- outer_bias: float32 [128], replicated, may hold values from -3 to 3
- pair_gain: float32 [128], replicated, may hold values from 0.5 to 1.5
- pair_shift: float32 [128], replicated, may hold values from -3 to 3
- up_weight: bfloat16 [128, 512], replicated, may hold values from -0.5 to 0.5
- up_bias: float32 [512], replicated, may hold values from -3 to 3
- down_weight: bfloat16 [512, 128], replicated, may hold values from -0.25 to 0.25
- down_bias: float32 [128], replicated, may hold values from -3 to 3
Outputs:
- pair_out: bfloat16 [256, 128, 128], P(('group', 'row')), parts along dimension 0
The draws below stay inside these ranges and needn't reach their ends.
There are 2 independent parts, one for each index of `group`. The reference program is written for one: setup_inputs(seed, part) draws one part's arguments, and reference() takes and returns one part's arrays. A program takes and returns all parts, laid end to end along the dimension named above; an argument that names none is the same for every part. Nothing has to cross between parts.
All inputs are finite; a program needn't handle non-finite values.
Results may differ from the reference program's by a relative error of at most 0.005.
Values may be sent and summed in bfloat16 or wider, within the bound.
A program may use at most 128 MiB of HBM per device.

```python
import jax
import jax.numpy as jnp
from jax import lax

SEQUENCE_COUNT = 128
ALIGN_CHANNELS = 256
PROJECT_WIDTH = 32
PAIR_W = 128
TRANS = 512
RESIDUE_COUNT = 128


def block_scale(rng, shape, pieces, smallest, high):
    def one(position, parts):
        heights = jax.random.uniform(jax.random.fold_in(jax.random.fold_in(rng, 6), position), (parts,), jnp.float32, smallest / len(pieces), high / len(pieces))
        return jnp.repeat(jnp.exp(heights), shape[position] // parts).reshape((-1,) + (1,) * (len(shape) - position - 1))

    level = one(*pieces[0])
    for cut in pieces[1:]:
        level = level * one(*cut)
    return level


def centred(rng, dims, scale, reach, cuts=(), kind=jnp.bfloat16):
    loudness = block_scale(rng, dims, cuts, -0.22, 0.18) if cuts else 1.0
    values = jax.random.normal(rng, dims, jnp.float32) * scale * loudness
    return jnp.minimum(jnp.maximum(values, -reach), reach).astype(kind)


def setup_inputs(seed: int = 0, part: int = 0) -> dict:
    key_list = jax.random.split(jax.random.key(seed), 15)
    own_keys = jax.random.split(jax.random.fold_in(key_list[14], part), 15)
    return {
        "alignment": centred(own_keys[0], (SEQUENCE_COUNT, RESIDUE_COUNT, ALIGN_CHANNELS), 1.0, 6.0, ((0, 16),)),
        "pair_rep": centred(own_keys[1], (RESIDUE_COUNT, RESIDUE_COUNT, PAIR_W), 1.0, 6.0, ((0, 16),)),
        "alignment_norm_gain": jnp.clip(jax.random.uniform(key_list[2], (ALIGN_CHANNELS,), jnp.float32, 0.5, 1.5), 0.5, 1.5),
        "alignment_norm_offset": centred(key_list[3], (ALIGN_CHANNELS,), 0.5, 3.0, (), jnp.float32),
        "left_projection_weight": centred(key_list[4], (ALIGN_CHANNELS, PROJECT_WIDTH), ALIGN_CHANNELS ** -0.5, 0.375),
        "right_projection_weight": centred(key_list[5], (ALIGN_CHANNELS, PROJECT_WIDTH), ALIGN_CHANNELS ** -0.5, 0.375),
        "outer_weight": centred(key_list[6], (PROJECT_WIDTH * PROJECT_WIDTH, PAIR_W), (2 * PROJECT_WIDTH) ** -0.5, 0.75),
        "outer_bias": centred(key_list[7], (PAIR_W,), 0.5, 3.0, (), jnp.float32),
        "pair_gain": jnp.clip(jax.random.uniform(key_list[8], (PAIR_W,), jnp.float32, 0.5, 1.5), 0.5, 1.5),
        "pair_shift": centred(key_list[9], (PAIR_W,), 0.5, 3.0, (), jnp.float32),
        "up_weight": centred(key_list[10], (PAIR_W, TRANS), PAIR_W ** -0.5, 0.5),
        "up_bias": centred(key_list[11], (TRANS,), 0.5, 3.0, (), jnp.float32),
        "down_weight": centred(key_list[12], (TRANS, PAIR_W), TRANS ** -0.5, 0.25),
        "down_bias": centred(key_list[13], (PAIR_W,), 0.5, 3.0, (), jnp.float32),
    }


epsilon = 1e-05

def layer_norm(values, gain, shift):
    values = values.astype(jnp.float32)
    center = lax.optimization_barrier(jnp.mean(values, axis=-1, keepdims=True))
    spread = lax.optimization_barrier(jnp.mean(jnp.square(values - center), axis=-1, keepdims=True))
    return (values - center) * lax.rsqrt(spread + epsilon) * gain + shift

def pair_update(left_rows, right_rows, pair_tile, layer_params):
    outer_weight, outer_bias, pair_gain, pair_shift, up_weight, up_bias, down_weight, down_bias = layer_params
    rows_i = left_rows.shape[0]
    rows_j = right_rows.shape[0]
    width = outer_weight.shape[1]
    proj_w = left_rows.shape[2]
    seq_total = left_rows.shape[1]
    outer_mean = jnp.einsum('isc,jse->ijce', left_rows.astype(jnp.float32), right_rows.astype(jnp.float32)) * (1.0 / seq_total)
    outer_mean = outer_mean.astype(jnp.bfloat16).reshape(rows_i * rows_j, proj_w * proj_w)
    summed = pair_tile.reshape(rows_i * rows_j, width).astype(jnp.float32) + jnp.dot(outer_mean, outer_weight, preferred_element_type=jnp.float32) + outer_bias
    normed = layer_norm(summed, pair_gain, pair_shift).astype(jnp.bfloat16)
    hidden = jax.nn.relu(jnp.dot(normed, up_weight, preferred_element_type=jnp.float32) + up_bias).astype(jnp.bfloat16)
    result = summed + jnp.dot(hidden, down_weight, preferred_element_type=jnp.float32) + down_bias
    return result.astype(jnp.bfloat16).reshape(rows_i, rows_j, width)

def reference(alignment, pair_rep, alignment_norm_gain, alignment_norm_offset, left_projection_weight, right_projection_weight, outer_weight, outer_bias, pair_gain, pair_shift, up_weight, up_bias, down_weight, down_bias):
    normed = layer_norm(alignment, alignment_norm_gain, alignment_norm_offset).astype(jnp.bfloat16)
    left = jnp.einsum('src,cd->rsd', normed.astype(jnp.float32), left_projection_weight.astype(jnp.float32)).astype(jnp.bfloat16)
    right = jnp.einsum('src,cd->rsd', normed.astype(jnp.float32), right_projection_weight.astype(jnp.float32)).astype(jnp.bfloat16)
    layer_params = (outer_weight, outer_bias, pair_gain, pair_shift, up_weight, up_bias, down_weight, down_bias)
    residues = pair_rep.shape[0]
    block_rows = 16 if residues % 16 == 0 else residues
    block_total = residues // block_rows
    left_blocks = left.reshape(block_total, block_rows, left.shape[1], left.shape[2])
    pair_blocks = pair_rep.reshape(block_total, block_rows, residues, pair_rep.shape[2])

    def one_block(operands):
        return pair_update(operands[0], right, operands[1], layer_params)
    updated = lax.map(one_block, (left_blocks, pair_blocks))
    updated = updated.reshape(residues, residues, pair_rep.shape[2])
    return jnp.transpose(updated, (1, 0, 2))
```

```python
import functools

import jax
import jax.numpy as jnp
from jax import lax
from jax.experimental import pallas as pl
from jax.experimental.pallas import tpu as pltpu
from jax.sharding import PartitionSpec as P

epsilon = 1e-05
MESH = pl.DeviceIdType.MESH


def layer_norm(values, gain, shift):
    values = values.astype(jnp.float32)
    center = jnp.mean(values, axis=-1, keepdims=True)
    spread = jnp.mean(jnp.square(values - center), axis=-1, keepdims=True)
    return (values - center) * lax.rsqrt(spread + epsilon) * gain + shift


def project_both(normed, left_projection_weight, right_projection_weight):
    left = jnp.einsum(
        "src,cd->rsd", normed, left_projection_weight, preferred_element_type=jnp.float32
    ).astype(jnp.bfloat16)
    right = jnp.einsum(
        "src,cd->rsd", normed, right_projection_weight, preferred_element_type=jnp.float32
    ).astype(jnp.bfloat16)
    return (left, right)


def pair_update(left_flat, right_flat, pair_tile, layer_params, proj_w):
    outer_weight, outer_bias, pair_gain, pair_shift, up_weight, up_bias, down_weight, down_bias = (
        layer_params
    )
    rows_i = left_flat.shape[0]
    rows_j = right_flat.shape[0]
    width = outer_weight.shape[1]
    seq_total = left_flat.shape[1] // proj_w
    left_rows = left_flat.reshape(rows_i, seq_total, proj_w)
    right_rows = right_flat.reshape(rows_j, seq_total, proj_w)
    outer_mean = jnp.einsum(
        "isc,jse->ijce", left_rows, right_rows, preferred_element_type=jnp.float32
    ) * (1.0 / seq_total)
    outer_mean = outer_mean.astype(jnp.bfloat16).reshape(rows_i * rows_j, proj_w * proj_w)
    summed = (
        pair_tile.reshape(rows_i * rows_j, width).astype(jnp.float32)
        + jnp.dot(outer_mean, outer_weight, preferred_element_type=jnp.float32)
        + outer_bias
    )
    normed = layer_norm(summed, pair_gain, pair_shift).astype(jnp.bfloat16)
    hidden = jax.nn.relu(
        jnp.dot(normed, up_weight, preferred_element_type=jnp.float32) + up_bias
    ).astype(jnp.bfloat16)
    result = summed + jnp.dot(hidden, down_weight, preferred_element_type=jnp.float32) + down_bias
    return result.astype(jnp.bfloat16).reshape(rows_i, rows_j, width)


def in_blocks(amount, builder):
    if amount > 256 and amount % 256 == 0:
        stacked = lax.map(
            lambda which_k: builder(which_k * 256, 256), jnp.arange(amount // 256, dtype=jnp.int32)
        )
        return stacked.reshape((amount,) + stacked.shape[2:])
    return builder(0, amount)


def shards(
    alignment,
    pair_rep,
    alignment_norm_gain,
    alignment_norm_offset,
    left_projection_weight,
    right_projection_weight,
    outer_weight,
    outer_bias,
    pair_gain,
    pair_shift,
    up_weight,
    up_bias,
    down_weight,
    down_bias,
):
    proj_w = left_projection_weight.shape[1]
    normed = layer_norm(alignment, alignment_norm_gain, alignment_norm_offset).astype(jnp.bfloat16)
    left, right = project_both(normed, left_projection_weight, right_projection_weight)
    left, right = (
        lax.all_to_all(left, "row", split_axis=0, concat_axis=1, tiled=True),
        lax.all_to_all(right, "row", split_axis=0, concat_axis=1, tiled=True),
    )
    left = left.reshape(left.shape[0], -1)
    right = right.reshape(right.shape[0], -1)
    layer_params = (
        outer_weight,
        outer_bias,
        pair_gain,
        pair_shift,
        up_weight,
        up_bias,
        down_weight,
        down_bias,
    )
    pieces = lax.all_gather(right, "row", axis=0, tiled=True)
    offset = jnp.int32(0)

    def builder(inner_start, amount):
        segment = lax.dynamic_slice_in_dim(pieces, inner_start, amount, 0)
        pair_tile = lax.dynamic_slice_in_dim(pair_rep, offset + inner_start, amount, 1)
        return jnp.transpose(pair_update(left, segment, pair_tile, layer_params, proj_w), (1, 0, 2))

    columns = in_blocks(pieces.shape[0], builder)
    return lax.all_to_all(columns, "row", split_axis=0, concat_axis=1, tiled=True)


def fused_kernel(
    n,
    align_ref,
    pair_ref,
    gain_ref,
    offset_ref,
    left_w_ref,
    right_w_ref,
    outer_w_ref,
    outer_b_ref,
    pair_gain_ref,
    pair_shift_ref,
    up_ref,
    up_b_ref,
    down_ref,
    down_b_ref,
    out_ref,
    norm_s,
    left_s,
    right_s,
    right_send,
    left_all,
    right_all,
    pair_all,
    pair_f,
    outer_s,
    outer_wt,
    own_sem,
    left_send_sem,
    left_sem,
    right_send_sem,
    right_sem,
    pair_send_sem,
    pair_sem,
):
    me = lax.axis_index("row")
    seqs, residues, channels = align_ref.shape
    proj = left_w_ref.shape[1]
    own = residues // n
    lanes = 128
    fold = lanes // proj
    groups = own // fold
    width = outer_w_ref.shape[1]
    f32, bf16 = jnp.float32, jnp.bfloat16

    barrier = pltpu.get_barrier_semaphore()
    for k in range(1, n):
        pl.semaphore_signal(barrier, inc=1, device_id={"row": lax.rem(me + k, n)}, device_id_type=MESH)

    def remote(src, dst, send, recv, device):
        return pltpu.make_async_remote_copy(
            src_ref=src, dst_ref=dst, send_sem=send, recv_sem=recv,
            device_id={"row": device}, device_id_type=MESH,
        )

    def row(ref):
        return ref[...].reshape(1, ref.shape[0])

    gain, offset = row(gain_ref), row(offset_ref)
    for s in range(seqs):
        normed = layer_norm(align_ref[s], gain, offset)
        for h in range(channels // lanes):
            norm_s[h, pl.ds(s * residues, residues), :] = normed[:, h * lanes : (h + 1) * lanes]
        left = lax.dot_general(
            left_w_ref[...], normed.astype(bf16), (((0,), (1,)), ((), ())), preferred_element_type=f32
        )
        left_s[pl.ds(s, proj, stride=seqs), :] = left
    left_all[me] = left_s[...].reshape(proj, seqs, residues).astype(bf16)
    parts = []
    rows = seqs * residues // fold
    for q in range(fold):
        part = jnp.concatenate(
            [norm_s[h, pl.ds(q, rows, stride=fold), :] for h in range(channels // lanes)], axis=1
        ).astype(bf16)
        parts.append(jnp.dot(part, right_w_ref[...], preferred_element_type=f32))
    right_s[...] = jnp.concatenate(parts, axis=1)
    for g in range(residues // fold):
        right_send[g] = right_s[pl.ds(g, seqs, stride=residues // fold), :].astype(bf16)

    pl.semaphore_wait(barrier, n - 1)

    near = me + 1 - 2 * lax.rem(me, 2)
    across = me + 2 - 4 * lax.rem(me // 2, 2)
    sends = []

    def send_left(src, device):
        copy = remote(
            left_all.at[src], left_all.at[src], left_send_sem.at[len(sends)], left_sem.at[src], device
        )
        copy.start()
        sends.append(copy)

    def wait_left(src):
        remote(left_all.at[src], left_all.at[src], left_send_sem.at[0], left_sem.at[src], me).wait_recv()

    for k in range(1, n // 4):
        send_left(me, lax.rem(me + 4 * k, n))
    send_left(me, across)
    send_left(me, near)
    rights, pairs = [], []
    for k in range(1, n):
        peer = lax.rem(me + k, n)
        copy = remote(
            right_send.at[pl.ds(peer * groups, groups)], right_all.at[me],
            right_send_sem.at[k], right_sem.at[me], peer,
        )
        copy.start()
        rights.append(copy)
    own_right = pltpu.make_async_copy(
        right_send.at[pl.ds(me * groups, groups)], right_all.at[me], own_sem.at[0]
    )
    own_right.start()
    for k in range(1, n):
        peer = lax.rem(me + k, n)
        copy = remote(pair_ref.at[:, peer], pair_all.at[me], pair_send_sem.at[k], pair_sem.at[me], peer)
        copy.start()
        pairs.append(copy)
    own_pair = pltpu.make_async_copy(pair_ref.at[:, me], pair_all.at[me], own_sem.at[1])
    own_pair.start()

    outer_wt[...] = outer_w_ref[...].astype(f32).T.astype(bf16)

    for k in range(1, n // 4):
        src = lax.rem(me + 4 * k, n)
        wait_left(src)
        send_left(src, across)
        send_left(src, near)
    for k in range(n // 4):
        src = lax.rem(across + 4 * k, n)
        wait_left(src)
        send_left(src, near)
    own_right.wait()
    for k in range(1, n):
        src = lax.rem(me + k, n)
        remote(right_all.at[src], right_all.at[src], right_send_sem.at[k], right_sem.at[src], me).wait_recv()
    right = jnp.concatenate(
        [right_all[:, g].reshape(n * seqs, lanes) for g in range(groups)], axis=1
    )
    right_t = right.astype(f32).T.astype(bf16)
    for k in range(n // 4):
        for start in (near, near + across - me):
            wait_left(lax.rem(start + 4 * k, n))

    scale = 1.0 / (n * seqs)
    for c in range(0, proj, 2):
        both = jnp.concatenate(
            [left_all[:, c + d].reshape(n * seqs, residues) for d in range(2)], axis=1
        )
        outer = (jnp.dot(right_t, both, preferred_element_type=f32) * scale).astype(bf16)
        for d in range(2):
            for j in range(own):
                outer_s[(c + d) * proj : (c + d + 1) * proj, j * residues : (j + 1) * residues] = outer[
                    j * proj : (j + 1) * proj, d * residues : (d + 1) * residues
                ]

    own_pair.wait()
    for k in range(1, n):
        src = lax.rem(me + k, n)
        remote(pair_all.at[src], pair_all.at[src], pair_send_sem.at[k], pair_sem.at[src], me).wait_recv()
    pair_f[...] = pair_all[...].astype(f32).reshape(pair_f.shape)

    for j in range(0, own, 2):
        summed_t = jnp.dot(
            outer_wt[...], outer_s[:, j * residues : (j + 2) * residues], preferred_element_type=f32
        )
        for d in range(2):
            summed = (
                summed_t[:, d * residues : (d + 1) * residues].T
                + pair_f[pl.ds(j + d, residues, stride=own), :]
                + row(outer_b_ref)
            )
            normed = layer_norm(summed, row(pair_gain_ref), row(pair_shift_ref)).astype(bf16)
            hidden = jax.nn.relu(
                jnp.dot(normed, up_ref[...], preferred_element_type=f32) + row(up_b_ref)
            ).astype(bf16)
            result = summed + jnp.dot(hidden, down_ref[...], preferred_element_type=f32) + row(down_b_ref)
            out_ref[j + d] = result.astype(bf16)

    for copy in sends + rights + pairs:
        copy.wait_send()


def fused(n, alignment, pair_rep, *params):
    seqs, residues, channels = alignment.shape
    own = pair_rep.shape[0]
    width = pair_rep.shape[2]
    proj = params[2].shape[1]
    lanes = 128
    groups = own * proj // lanes
    f32, bf16 = jnp.float32, jnp.bfloat16
    vmem = pl.BlockSpec(memory_space=pltpu.VMEM)
    return pl.pallas_call(
        functools.partial(fused_kernel, n),
        out_shape=jax.ShapeDtypeStruct((own, residues, width), bf16),
        in_specs=[vmem, pl.BlockSpec(memory_space=pl.ANY)] + [vmem] * len(params),
        out_specs=vmem,
        scratch_shapes=[
            pltpu.VMEM((channels // lanes, seqs * residues, lanes), f32),
            pltpu.VMEM((proj * seqs, residues), f32),
            pltpu.VMEM((seqs * residues * proj // lanes, lanes), f32),
            pltpu.VMEM((residues * proj // lanes, seqs, lanes), bf16),
            pltpu.VMEM((n, proj, seqs, residues), bf16),
            pltpu.VMEM((n, groups, seqs, lanes), bf16),
            pltpu.VMEM((n, own, own, width), bf16),
            pltpu.VMEM((residues * own, width), f32),
            pltpu.VMEM((proj * proj, own * residues), bf16),
            pltpu.VMEM((width, proj * proj), bf16),
            pltpu.SemaphoreType.DMA((2,)),
            pltpu.SemaphoreType.DMA((n,)),
            pltpu.SemaphoreType.DMA((n,)),
            pltpu.SemaphoreType.DMA((n,)),
            pltpu.SemaphoreType.DMA((n,)),
            pltpu.SemaphoreType.DMA((n,)),
            pltpu.SemaphoreType.DMA((n,)),
        ],
        compiler_params=pltpu.CompilerParams(collective_id=0, has_side_effects=True),
    )(alignment, pair_rep.reshape(own, n, residues // n, width), *params)


def fits(n, alignment, pair_rep, left_w):
    seqs, residues = alignment.shape[:2]
    own, width = pair_rep.shape[0], pair_rep.shape[2]
    proj = left_w.shape[1]
    return (
        n % 4 == 0
        and seqs == 8
        and residues == 128
        and width == 128
        and own == 8
        and alignment.shape[2] % 128 == 0
        and proj % 32 == 0
        and 128 % proj == 0
    )


def dispatch(n, *args):
    if fits(n, args[0], args[1], args[4]):
        return fused(n, *args)
    return shards(*args)


def solution(mesh):
    placed = (
        P(("group", "row"), None, None),
        P(("group", "row"), None, None),
        P(),
        P(),
        P(),
        P(),
        P(),
        P(),
        P(),
        P(),
        P(),
        P(),
        P(),
        P(),
    )
    return jax.shard_map(
        functools.partial(dispatch, mesh.shape["row"]),
        mesh=mesh,
        in_specs=placed,
        out_specs=P(("group", "row"), None, None),
        check_vma=False,
    )
```
